32 devices in a mesh: ctx: 8 (over y, x, core), tp: 4 (over z).
Axes of the slice: x: 2, y: 2, z: 4, core: 2. Of those that a mesh axis runs over, the one named last changes fastest.
Arguments:
- tokens: bfloat16 [2, 1024, 2048], P(None, 'ctx'), may hold values from -8 to 8
- attn_gain: float32 [2048], replicated, may hold values from 0.5 to 1.6
- w_query: bfloat16 [2048, 2048], P(None, 'tp'), may hold values from -1 to 1
- w_key: bfloat16 [2048, 2048], P(None, 'tp')
- w_value: bfloat16 [2048, 2048], P(None, 'tp'), may hold values from -0.125 to 0.125
- w_out: bfloat16 [2048, 2048], P('tp'), may hold values from -0.5 to 0.5
- ffn_gain: float32 [2048], replicated, may hold values from 0.5 to 1.5
- w_gate: bfloat16 [2048, 8192], P(None, 'tp'), may hold values from -0.125 to 0.125
- w_up: bfloat16 [2048, 8192], P(None, 'tp'), may hold values from -0.125 to 0.125
- w_down: bfloat16 [8192, 2048], P('tp'), may hold values from -0.0625 to 0.0625
- cotangent: bfloat16 [2, 1024, 2048], P(None, 'ctx'), may hold values from -6 to 6
Outputs:
- output: bfloat16 [2, 1024, 2048], P(None, 'ctx')
- d_tokens: float32 [2, 1024, 2048], P(None, 'ctx')
- d_attn_gain: float32 [2048], P('ctx')
- d_query: float32 [2048, 2048], P('ctx', 'tp')
- d_key: float32 [2048, 2048], P('ctx', 'tp')
- d_value: float32 [2048, 2048], P('ctx', 'tp')
- d_out: float32 [2048, 2048], P('tp', 'ctx')
- d_ffn_gain: float32 [2048], P('ctx')
- d_gate: float32 [2048, 8192], P('ctx', 'tp')
- d_up: float32 [2048, 8192], P('ctx', 'tp')
- d_down: float32 [8192, 2048], P('tp', 'ctx')
The draws below stay inside these ranges and needn't reach their ends.
All inputs are finite; a program needn't handle non-finite values.
Results may differ from the reference program's by a relative error of at most 0.025.
Values may be sent and summed in bfloat16 or wider, within the bound.
No kernel may reach another device: no remote copies, remote signals or barrier semaphores. Data moves between devices by JAX's collectives and lax.ppermute only.
A program may use at most 256 MiB of HBM per device.

```python
import jax
import jax.numpy as jnp
from jax import lax

D = 2048
HEADS = 32
HEAD_DIM = 64
FF = 8192
SEQS = 2
LENGTH = 1024


def draw_attn_gain(key, part):
    return jax.random.uniform(key, (D,), jnp.float32, 0.5, 1.5)


def draw_tokens(key, part):
    base = jax.random.truncated_normal(jax.random.fold_in(key, 201), -6.0, 6.0, (SEQS, LENGTH, D), jnp.float32)
    return base.astype(jnp.bfloat16)


def draw_w_query(key, part):
    base = jax.random.truncated_normal(jax.random.fold_in(key, 101), -6.0, 6.0, (D, HEADS * HEAD_DIM), jnp.float32) * D ** (-0.5)
    return base.astype(jnp.bfloat16)


def draw_w_key(key, part):
    fresh = jax.random.truncated_normal(jax.random.fold_in(key, 102), -6.0, 6.0, (D, HEADS * HEAD_DIM), jnp.float32) * D ** (-0.5)
    return fresh.astype(jnp.bfloat16)


def steps_of(key, dims, cuts, smallest, largest):
    gain, own = 1.0, jax.random.fold_in(key, 6)
    for dim, shards_of in cuts:
        steps = jnp.exp(jax.random.uniform(jax.random.fold_in(own, dim), (shards_of,), jnp.float32, smallest / len(cuts), largest / len(cuts)))
        gain = gain * jnp.repeat(steps, dims[dim] // shards_of).reshape([-1 if axis == dim else 1 for axis in range(len(dims))])
    return gain


def bell_draw(key, shape, scale, limit, cuts=(), kind=jnp.bfloat16):
    factor_of = steps_of(key, shape, cuts, -0.22, 0.18) if cuts else 1.0
    values = jax.random.normal(key, shape, jnp.float32) * scale * factor_of
    return jnp.minimum(jnp.maximum(values, -limit), limit).astype(kind)


def setup_inputs(seed: int = 0) -> dict:
    arg_keys = jax.random.split(jax.random.key(seed), 12)
    return {
        "tokens": draw_tokens(jax.random.fold_in(arg_keys[11], 71), 0),
        "attn_gain": draw_attn_gain(jax.random.fold_in(arg_keys[11], 71), 0),
        "w_query": draw_w_query(jax.random.fold_in(arg_keys[11], 71), 0),
        "w_key": draw_w_key(jax.random.fold_in(arg_keys[11], 71), 0),
        "w_value": bell_draw(arg_keys[4], (D, HEADS * HEAD_DIM), D ** -0.5, 0.125, ((1, 4),)),
        "w_out": bell_draw(arg_keys[5], (HEADS * HEAD_DIM, D), (D // 16) ** -0.5, 0.5, ((0, 4),)),
        "ffn_gain": jnp.clip(1.0 + 0.1 * jax.random.normal(arg_keys[6], (D,), jnp.float32), 0.5, 1.5),
        "w_gate": bell_draw(arg_keys[7], (D, FF), D ** -0.5, 0.125, ((1, 4),)),
        "w_up": bell_draw(arg_keys[8], (D, FF), D ** -0.5, 0.125, ((1, 4),)),
        "w_down": bell_draw(arg_keys[9], (FF, D), FF ** -0.5, 0.0625, ((0, 4),)),
        "cotangent": bell_draw(arg_keys[10], (SEQS, LENGTH, D), 1.0, 6.0, ((1, 8),)),
    }


EPS = 1e-05
THETA = 130000.0

@jax.custom_vjp
def low(v):
    return lax.optimization_barrier(v.astype(jnp.bfloat16)).astype(jnp.float32)

@jax.custom_vjp
def low_back(v):
    return v

def low_keep(v):
    return (low(v), None)

def low_pass(kept, grad):
    return (grad,)

def back_keep(v):
    return (v, None)

def back_low(kept, grad):
    return (low(grad),)
low.defvjp(low_keep, low_pass)
low_back.defvjp(back_keep, back_low)

def tables(length, dtype):
    half = HEAD_DIM // 2
    inverse = THETA ** (-(jnp.arange(half).astype(dtype) * 2.0 / HEAD_DIM))
    angle = jnp.arange(length).astype(dtype)[:, None] * inverse[None, :]
    angle = jnp.concatenate([angle, angle], axis=-1)
    return (jnp.cos(angle), jnp.sin(angle))

def rotate(t, cosine, sine):
    half = t.shape[-1] // 2
    turned = jnp.concatenate([-t[..., half:], t[..., :half]], axis=-1)
    return t * cosine[:, None, :] + turned * sine[:, None, :]

def project(left_operand, weight_matrix):
    return jnp.einsum('atg,gx->atx', left_operand, weight_matrix, precision=lax.Precision.HIGHEST)

def rms(h):
    return lax.rsqrt(lax.optimization_barrier(jnp.mean(h * h, axis=-1, keepdims=True)) + EPS)

def head_attend(triple):
    queries, keys, values = triple
    length = queries.shape[0]
    row_count = min(length, 1024)

    def one_block(pieces):
        query_block_rows, offset = pieces
        scores = low_back(jnp.dot(query_block_rows, keys.T, precision=lax.Precision.HIGHEST) * HEAD_DIM ** (-0.5))
        visible = jnp.arange(length)[None, :] <= (offset + jnp.arange(row_count))[:, None]
        scores = jnp.where(visible, scores, -jnp.inf)
        top = lax.optimization_barrier(jnp.max(scores, axis=-1, keepdims=True))
        layer_weights = jnp.exp(scores - top)
        total = lax.optimization_barrier(jnp.sum(layer_weights, axis=-1, keepdims=True))
        result = jnp.dot(low(layer_weights), values, precision=lax.Precision.HIGHEST) / total
        return low(low_back(result))
    offsets = (jnp.arange(length // row_count) * row_count).astype(jnp.int32)
    blocks = lax.map(jax.checkpoint(one_block), (queries.reshape(length // row_count, row_count, HEAD_DIM), offsets))
    return blocks.reshape(length, HEAD_DIM)

def forward(h, attn_gain, w_query, w_key, w_value, w_out, ffn_gain, w_gate, w_up, w_down):
    seqs, length, width = h.shape
    n1 = low(h * rms(h) * attn_gain)
    cosine, sine = tables(length, h.dtype)
    shape = (seqs, length, HEADS, HEAD_DIM)
    queries = low(rotate(low_back(project(n1, w_query)).reshape(shape), cosine, sine))
    keys = low(rotate(low_back(project(n1, w_key)).reshape(shape), cosine, sine))
    values = low(low_back(project(n1, w_value))).reshape(shape)

    def heads_first(t):
        return t.transpose(0, 2, 1, 3).reshape(seqs * HEADS, length, HEAD_DIM)
    result = lax.map(jax.checkpoint(head_attend), (heads_first(queries), heads_first(keys), heads_first(values)))
    attn = result.reshape(seqs, HEADS, length, HEAD_DIM).transpose(0, 2, 1, 3).reshape(seqs, length, HEADS * HEAD_DIM)
    h2 = h + low_back(project(attn, w_out))
    n2 = low(h2 * rms(h2) * ffn_gain)
    gate = low_back(project(n2, w_gate))
    up = low_back(project(n2, w_up))
    hidden_state = low(jax.nn.silu(gate) * up)
    return h2 + low_back(project(hidden_state, w_down))

def reference(tokens, attn_gain, w_query, w_key, w_value, w_out, ffn_gain, w_gate, w_up, w_down, cotangent):
    inputs = [left_operand.astype(jnp.float32) for left_operand in (tokens, attn_gain, w_query, w_key, w_value, w_out, ffn_gain, w_gate, w_up, w_down)]
    output, pull = jax.vjp(forward, *inputs)
    grads = pull(cotangent.astype(jnp.float32))
    return (output.astype(jnp.bfloat16), grads[0], grads[1], grads[2], grads[3], grads[4], grads[5], grads[6], grads[7], grads[8], grads[9])
```

```python
import jax
import jax.numpy as jnp
import numpy as np
from jax import lax
from jax.experimental import pallas as pl
from jax.experimental.pallas import tpu as pltpu
from jax.sharding import PartitionSpec as P

HEAD_DIM = 64
PAIR = 2 * HEAD_DIM
EPS = 1e-05
THETA = 130000.0
F32 = jnp.float32
BF16 = jnp.bfloat16


def swap(value, axis, bit):
    count = lax.axis_size(axis)
    return lax.ppermute(value, axis, [(i, i ^ bit) for i in range(count)])


def passed_along(value, axis, steps):
    count = lax.axis_size(axis)
    leading, last = (max(0, -steps), min(count, count - steps))
    return lax.ppermute(value, axis, [(source, source + steps) for source in range(leading, last)])


def shifted(block, axis, distance):
    devices = range(lax.axis_size(axis))
    route = [((i - distance) % len(devices), i) for i in devices]
    return lax.ppermute(block, axis, route)


def tables(positions):
    half = HEAD_DIM // 2
    inverse = THETA ** (-(jnp.arange(half).astype(jnp.float32) * 2.0 / HEAD_DIM))
    angle = positions.astype(jnp.float32)[:, None] * inverse[None, :]
    angle = jnp.concatenate([angle, angle], axis=-1)
    return (jnp.cos(angle), jnp.sin(angle))


def pair_tables(length):
    half = HEAD_DIM // 2
    inverse = np.float32(THETA) ** (-(np.arange(half, dtype=np.float32) * 2.0 / HEAD_DIM))
    angle = np.arange(length, dtype=np.float32)[:, None] * inverse.astype(np.float32)[None, :]
    cosine, sine = np.cos(angle).astype(np.float32), np.sin(angle).astype(np.float32)
    return (
        np.concatenate([cosine] * 4, axis=-1),
        np.concatenate([-sine, sine, -sine, sine], axis=-1),
    )


def rotate(t, cosine, sine):
    half = t.shape[-1] // 2
    turned = jnp.concatenate([-t[..., half:], t[..., :half]], axis=-1)
    return t * cosine[:, None, :] + turned * sine[:, None, :]


def unrotate(grad, cosine, sine):
    half = grad.shape[-1] // 2
    scaled = grad * sine[:, None, :]
    return grad * cosine[:, None, :] + jnp.concatenate(
        [scaled[..., half:], -scaled[..., :half]], axis=-1
    )


def rms(h):
    return lax.rsqrt(jnp.mean(h * h, axis=-1, keepdims=True) + EPS)


def outer(left, right):
    return lax.dot_general(
        left, right, (((0,), (0,)), ((), ())), preferred_element_type=jnp.float32
    )


def by_transpose(left, weight):
    return lax.dot_general(
        left, weight, (((1,), (1,)), ((), ())), preferred_element_type=jnp.float32
    )


def tp_bits():
    count = lax.axis_size("tp")
    return [1 << b for b in range(count.bit_length() - 1)]


def tp_sum(chunks):
    index = lax.axis_index("tp")
    bits = tp_bits()
    chunks = list(chunks)
    for bit in bits:
        upper = (index & bit) != 0
        sent = []
        for x in chunks:
            half = x.shape[0] // 2
            lo, hi = x[:half], x[half:]
            sent.append((jnp.where(upper, lo, hi), jnp.where(upper, hi, lo)))
        got = [swap(s, "tp", bit) for s, _ in sent]
        chunks = [
            (k.astype(F32) + r.astype(F32)).astype(BF16) for (_, k), r in zip(sent, got)
        ]
    for bit in reversed(bits):
        upper = (index & bit) != 0
        got = [swap(x, "tp", bit) for x in chunks]
        chunks = [
            jnp.concatenate([jnp.where(upper, r, x), jnp.where(upper, x, r)], axis=0)
            for x, r in zip(chunks, got)
        ]
    return chunks


def gather_rows(x):
    near = swap(x, "ctx", 1)
    far = swap(x, "ctx", 2)
    return [x, near, far, swap(far, "ctx", 1)]


def column_piece(x, slot):
    count = lax.axis_size("ctx")
    width = x.shape[1] // count
    if count <= 8:
        pieces = [x[:, k * width : (k + 1) * width] for k in range(count)]
        return lax.select_n(slot, *pieces)
    return lax.dynamic_slice_in_dim(x, slot * width, width, axis=1)


def gather_columns(x):
    count = lax.axis_size("ctx")
    index = lax.axis_index("ctx")
    q, high = index & 3, index >> 2

    def columns(k):
        return jnp.concatenate(
            [column_piece(x, ((high ^ r) << 2) | (q ^ k)) for r in range(count // 4)], axis=1
        )

    near = swap(columns(1), "ctx", 1)
    far = swap(jnp.concatenate([columns(2), columns(3)], axis=1), "ctx", 2)
    mine = far.shape[1] // 2
    return [columns(0), near, far[:, :mine], swap(far[:, mine:], "ctx", 1)]


def sum_upper(total, dim):
    bit = lax.axis_size("ctx") // 2
    while bit >= 4:
        half = total.shape[dim] // 2
        keep = lax.slice_in_dim(total, 0, half, axis=dim)
        send = lax.slice_in_dim(total, half, 2 * half, axis=dim).astype(BF16)
        total = keep + swap(send, "ctx", bit).astype(F32)
        bit //= 2
    return total


def grad_rows(slices, rows):
    total = outer(jnp.concatenate(slices, axis=0), jnp.concatenate(rows, axis=0))
    return sum_upper(total, 0)


def grad_columns(rows, slices):
    total = outer(jnp.concatenate(rows, axis=0), jnp.concatenate(slices, axis=0))
    return sum_upper(total, 1)


def sum_everywhere(x):
    for bit in tp_bits():
        x = x + swap(x, "tp", bit)
    count = lax.axis_size("ctx")
    for b in range(count.bit_length() - 1):
        x = x + swap(x, "ctx", 1 << b)
    return x


def turn(t):
    lane = lax.broadcasted_iota(jnp.int32, t.shape, 1)
    left = pltpu.roll(t, PAIR - HEAD_DIM // 2, 1)
    right = pltpu.roll(t, HEAD_DIM // 2, 1)
    return jnp.where(lane % HEAD_DIM < HEAD_DIM // 2, left, right)


def dot_t(a, b):
    return lax.dot_general(a, b, (((1,), (1,)), ((), ())), preferred_element_type=F32)


def dot_0(a, b):
    return lax.dot_general(a, b, (((0,), (0,)), ((), ())), preferred_element_type=F32)


def head_lanes(x, head):
    lane = lax.broadcasted_iota(jnp.int32, x.shape, 1)
    return jnp.where(lane // HEAD_DIM == head, x, jnp.zeros_like(x))


def causal(scores, start):
    row = lax.broadcasted_iota(jnp.int32, scores.shape, 0) + start
    column = lax.broadcasted_iota(jnp.int32, scores.shape, 1)
    return jnp.where(column <= row, scores, -jnp.inf)


def attend_kernel(x_ref, o_ref, wide_ref, lse_ref, *, step):
    length = x_ref.shape[0]
    for b in range(length // step):
        start, stop = b * step, (b + 1) * step
        q = x_ref[start:stop, 0:PAIR] * BF16(HEAD_DIM ** (-0.5))
        k = x_ref[0:stop, PAIR : 2 * PAIR]
        v = x_ref[0:stop, 2 * PAIR : 3 * PAIR]
        total = jnp.zeros((step, PAIR), F32)
        logs = []
        for head in range(2):
            scores = causal(dot_t(head_lanes(q, head), k), start)
            top = jnp.max(scores, axis=-1, keepdims=True)
            weights = jnp.exp(scores - top)
            mass = jnp.sum(weights, axis=-1, keepdims=True)
            value = jnp.dot(weights.astype(BF16), v, preferred_element_type=F32) / mass
            total = total + head_lanes(value, head)
            logs.append(top + jnp.log(mass))
        wide_ref[start:stop, :] = total
        o_ref[start:stop, :] = total.astype(BF16)
        lane = lax.broadcasted_iota(jnp.int32, (step, PAIR), 1)
        lse_ref[start:stop, :] = jnp.where(lane < HEAD_DIM, logs[0], logs[1])


def attend(x):
    length = x.shape[0]
    step = min(256, length)
    flops = 2 * 2 * 2 * length * length * PAIR // 2
    return pl.pallas_call(
        lambda *refs: attend_kernel(*refs, step=step),
        out_shape=(
            jax.ShapeDtypeStruct((length, PAIR), BF16),
            jax.ShapeDtypeStruct((length, PAIR), F32),
            jax.ShapeDtypeStruct((length, PAIR), F32),
        ),
        cost_estimate=pl.CostEstimate(
            flops=flops, bytes_accessed=length * PAIR * 16, transcendentals=length * length
        ),
        name="attend",
    )(x)


def attend_back_kernel(x_ref, do_ref, wide_ref, lse_ref, cos_ref, sin_ref, g_ref, dk_ref, dv_ref, *, step):
    length = x_ref.shape[0]
    scale = HEAD_DIM ** (-0.5)
    dk_ref[...] = jnp.zeros_like(dk_ref)
    dv_ref[...] = jnp.zeros_like(dv_ref)
    for b in range(length // step):
        start, stop = b * step, (b + 1) * step
        q = x_ref[start:stop, 0:PAIR] * BF16(scale)
        k = x_ref[0:stop, PAIR : 2 * PAIR]
        v = x_ref[0:stop, 2 * PAIR : 3 * PAIR]
        do = do_ref[start:stop, :]
        product = do.astype(F32) * wide_ref[start:stop, :]
        dq = jnp.zeros((step, PAIR), F32)
        for head in range(2):
            q_h, do_h = head_lanes(q, head), head_lanes(do, head)
            delta = jnp.sum(head_lanes(product, head), axis=-1, keepdims=True)
            lse = lse_ref[start:stop, head * HEAD_DIM : head * HEAD_DIM + 1]
            scores = causal(dot_t(q_h, k), start)
            probs = jnp.exp(scores - lse)
            d_probs = dot_t(do_h, v)
            d_scores = (probs * (d_probs - delta)).astype(BF16)
            dq = dq + head_lanes(jnp.dot(d_scores, k, preferred_element_type=F32), head)
            dk_ref[0:stop, :] += dot_0(d_scores, q_h)
            dv_ref[0:stop, :] += dot_0(probs.astype(BF16), do_h)
        dq = dq * scale
        g_ref[start:stop, 0:PAIR] = (
            dq * cos_ref[start:stop, :] - turn(dq) * sin_ref[start:stop, :]
        ).astype(BF16)
    for b in range(length // step):
        start, stop = b * step, (b + 1) * step
        dk = dk_ref[start:stop, :]
        g_ref[start:stop, PAIR : 2 * PAIR] = (
            dk * cos_ref[start:stop, :] - turn(dk) * sin_ref[start:stop, :]
        ).astype(BF16)
        g_ref[start:stop, 2 * PAIR : 3 * PAIR] = dv_ref[start:stop, :].astype(BF16)


def attend_back(x, do, wide, lse, cosine, sine):
    length = x.shape[0]
    step = min(256, length)
    flops = 5 * 2 * 2 * length * length * PAIR // 2
    return pl.pallas_call(
        lambda *refs: attend_back_kernel(*refs, step=step),
        out_shape=jax.ShapeDtypeStruct((length, 3 * PAIR), BF16),
        scratch_shapes=[pltpu.VMEM((length, PAIR), F32), pltpu.VMEM((length, PAIR), F32)],
        cost_estimate=pl.CostEstimate(
            flops=flops, bytes_accessed=length * PAIR * 30, transcendentals=length * length
        ),
        name="attend_back",
    )(x, do, wide, lse, cosine, sine)


def score_block(queries, keys, q_start, k_start):
    scores = jnp.einsum(
        "sqhd,skhd->shqk", queries, keys, preferred_element_type=jnp.float32
    ) * HEAD_DIM ** (-0.5)
    q_pos = q_start + jnp.arange(queries.shape[1])
    k_pos = k_start + jnp.arange(keys.shape[1])
    return jnp.where(k_pos[None, :] <= q_pos[:, None], scores, -jnp.inf)


def grad_block(queries, grads_out, log_total, delta, keys, values, q_start, k_start):
    scores = score_block(queries, keys, q_start, k_start)
    probs = jnp.exp(scores - log_total[..., None])
    d_probs = jnp.einsum("sqhd,skhd->shqk", grads_out, values, preferred_element_type=jnp.float32)
    d_scores = (probs * (d_probs - delta[..., None])).astype(jnp.bfloat16)
    scale = HEAD_DIM ** (-0.5)
    d_queries = (
        jnp.einsum("shqk,skhd->sqhd", d_scores, keys, preferred_element_type=jnp.float32) * scale
    )
    d_keys = (
        jnp.einsum("shqk,sqhd->skhd", d_scores, queries, preferred_element_type=jnp.float32) * scale
    )
    d_values = jnp.einsum(
        "shqk,sqhd->skhd", probs.astype(jnp.bfloat16), grads_out, preferred_element_type=jnp.float32
    )
    return (d_queries, d_keys, d_values)


def ring_forward(qp, kp, vp, shape):
    seqs, block, local_heads, _ = shape
    device_index = lax.axis_index("ctx")
    count = lax.axis_size("ctx")
    start = device_index * block
    cosine, sine = tables(start + jnp.arange(block))
    queries = rotate(qp.reshape(shape), cosine, sine).astype(jnp.bfloat16)
    keys = rotate(kp.reshape(shape), cosine, sine).astype(jnp.bfloat16)
    values = vp.astype(jnp.bfloat16).reshape(shape)

    def forward_step(state, pair, step):
        run_max, total, accum = state
        source = (device_index - step) % count
        scores = score_block(queries, pair[0], start, source * block)
        new_max = jnp.maximum(run_max, jnp.max(scores, axis=-1))
        fade = jnp.exp(run_max - new_max)
        layer_weights = jnp.exp(scores - new_max[..., None])
        total = total * fade + jnp.sum(layer_weights, axis=-1)
        accum = accum * fade[..., None] + jnp.einsum(
            "shqk,skhd->shqd",
            layer_weights.astype(jnp.bfloat16),
            pair[1],
            preferred_element_type=jnp.float32,
        )
        return (new_max, total, accum)

    def cycle_step(step, carry):
        pair, state = carry
        new_state = lax.cond(
            step <= device_index, lambda: forward_step(state, pair, step), lambda: state
        )
        pair = passed_along(pair, "ctx", 1)
        return (pair, new_state)

    state_zero = (
        jnp.full((seqs, local_heads, block), -jnp.inf, jnp.float32),
        jnp.zeros((seqs, local_heads, block), jnp.float32),
        jnp.zeros((seqs, local_heads, block, HEAD_DIM), jnp.float32),
    )
    pair, state = lax.fori_loop(
        0, count - 1, cycle_step, (jnp.stack([keys, values]), state_zero)
    )
    run_max, total, accum = lax.cond(
        count - 1 <= device_index, lambda: forward_step(state, pair, count - 1), lambda: state
    )
    result = accum / total[..., None]
    log_total = run_max + jnp.log(total)
    attn = result.astype(jnp.bfloat16).transpose(0, 2, 1, 3)
    attn = attn.reshape(seqs * block, local_heads * HEAD_DIM)
    return attn, (queries, keys, values, result, log_total, cosine, sine)


def ring_backward(do, saved):
    queries, keys, values, result, log_total, cosine, sine = saved
    shape = queries.shape
    device_index = lax.axis_index("ctx")
    count = lax.axis_size("ctx")
    block = shape[1]
    start = device_index * block
    grads_out = do.reshape(shape)
    delta = jnp.sum(grads_out.astype(jnp.float32).transpose(0, 2, 1, 3) * result, axis=-1)

    def back_step(step, carry):
        pack, stats, d_q, key_grads = carry
        source = (device_index - step) % count
        useful = jnp.logical_or(step == 0, step > device_index)

        def work():
            part_q, part_k, value_portion = grad_block(
                pack[0], pack[1], stats[0], stats[1], keys, values, source * block, start
            )
            return (d_q + part_q, key_grads + jnp.stack([part_k, value_portion]))

        new_d_q, new_grads = lax.cond(useful, work, lambda: (d_q, key_grads))
        pack = shifted(pack, "ctx", 1)
        stats = shifted(stats, "ctx", 1)
        new_d_q = shifted(new_d_q.astype(jnp.bfloat16), "ctx", 1).astype(new_d_q.dtype)
        return (pack, stats, new_d_q, new_grads)

    carry_zero = (
        jnp.stack([queries, grads_out]),
        jnp.stack([log_total, delta]),
        jnp.zeros(shape, jnp.float32),
        jnp.zeros((2,) + shape, jnp.float32),
    )
    pack, stats, d_q, grads = lax.fori_loop(0, count, back_step, carry_zero)
    flat = (shape[0] * block, shape[2] * HEAD_DIM)
    return (
        unrotate(d_q, cosine, sine).astype(jnp.bfloat16).reshape(flat),
        unrotate(grads[0], cosine, sine).astype(jnp.bfloat16).reshape(flat),
        grads[1].astype(jnp.bfloat16).reshape(flat),
    )


def to_pairs(parts, seqs, block):
    pairs = parts[0].shape[1] // PAIR
    cut = [p.reshape(seqs, block, pairs, PAIR).transpose(0, 2, 1, 3) for p in parts]
    sent = jnp.concatenate(cut, axis=-1).reshape(seqs * pairs * block, len(parts) * PAIR)
    return lax.all_to_all(sent, "ctx", 0, 0, tiled=True)


def from_pairs(x, seqs, block, parts):
    got = lax.all_to_all(x, "ctx", 0, 0, tiled=True)
    pairs = got.shape[0] // (seqs * block)
    got = got.reshape(seqs, pairs, block, parts * PAIR)
    return [
        got[..., k * PAIR : (k + 1) * PAIR]
        .transpose(0, 2, 1, 3)
        .reshape(seqs * block, pairs * PAIR)
        for k in range(parts)
    ]


def per_device(
    tokens, attn_gain, w_query, w_key, w_value, w_out, ffn_gain, w_gate, w_up, w_down, cotangent
):
    seqs, block, width = tokens.shape
    local_width = w_query.shape[1]
    local_heads = local_width // HEAD_DIM
    rows = seqs * block
    device_index = lax.axis_index("ctx")
    count = lax.axis_size("ctx")
    start = device_index * block
    by_pairs = seqs * (local_width // PAIR) == count
    h_flat = tokens.astype(jnp.float32).reshape(rows, width)
    scale_one = rms(h_flat)
    n1 = (h_flat * scale_one * attn_gain).astype(jnp.bfloat16)
    qp = jnp.dot(n1, w_query, preferred_element_type=jnp.float32)
    kp = jnp.dot(n1, w_key, preferred_element_type=jnp.float32)
    vp = jnp.dot(n1, w_value, preferred_element_type=jnp.float32)
    if by_pairs:
        cosine, sine = (jnp.asarray(t) for t in pair_tables(count * block))
        c_own = lax.dynamic_slice_in_dim(cosine, start, block, axis=0)[None, :, None, :HEAD_DIM]
        s_own = lax.dynamic_slice_in_dim(sine, start, block, axis=0)[None, :, None, :HEAD_DIM]

        def rope(t):
            t = t.reshape(seqs, block, local_heads, HEAD_DIM)
            half = HEAD_DIM // 2
            other = jnp.concatenate([t[..., half:], t[..., :half]], axis=-1)
            return (t * c_own + other * s_own).astype(BF16).reshape(rows, local_width)

        triple = to_pairs([rope(qp), rope(kp), vp.astype(BF16)], seqs, block)
        attn_own, attn_wide, lse = attend(triple)
        (attn,) = from_pairs(attn_own, seqs, block, 1)
    else:
        attn, saved = ring_forward(qp, kp, vp, (seqs, block, local_heads, HEAD_DIM))
    a_part = jnp.dot(attn, w_out, preferred_element_type=jnp.float32).astype(BF16)
    a_sum = tp_sum([a_part[s * block : (s + 1) * block] for s in range(seqs)])

    grad_in = cotangent.reshape(rows, width)
    d_hidden = by_transpose(grad_in, w_down)
    g_slices = gather_columns(grad_in)
    n1_slices = gather_columns(n1)
    attn_rows = gather_rows(attn)

    h2 = h_flat + jnp.concatenate(a_sum, axis=0).astype(F32)
    scale_two = rms(h2)
    n2 = (h2 * scale_two * ffn_gain).astype(jnp.bfloat16)
    n2_slices = gather_columns(n2)
    gate = jnp.dot(n2, w_gate, preferred_element_type=jnp.float32)
    up = jnp.dot(n2, w_up, preferred_element_type=jnp.float32)
    sigma = jax.nn.sigmoid(gate)
    swish = gate * sigma
    hidden_state = (swish * up).astype(jnp.bfloat16)
    d_gate_act = (d_hidden * up * sigma * (1.0 + gate * (1.0 - sigma))).astype(jnp.bfloat16)
    d_up_act = (d_hidden * swish).astype(jnp.bfloat16)
    d_n2_part = (by_transpose(d_gate_act, w_gate) + by_transpose(d_up_act, w_up)).astype(BF16)
    d_n2_sum = tp_sum([d_n2_part[s * block : (s + 1) * block] for s in range(seqs)])

    g_down = grad_columns(gather_rows(hidden_state), g_slices)
    g_gate = grad_rows(n2_slices, gather_rows(d_gate_act))
    g_up = grad_rows(n2_slices, gather_rows(d_up_act))

    d_n2 = jnp.concatenate(d_n2_sum, axis=0).astype(F32)
    g_ffn_gain = jnp.sum(d_n2 * h2 * scale_two, axis=0)
    scaled_two = d_n2 * ffn_gain
    d_h2 = (
        grad_in.astype(F32)
        + scale_two * scaled_two
        - h2 * scale_two**3 * jnp.mean(scaled_two * h2, axis=-1, keepdims=True)
    )
    branch_gradient = d_h2.astype(jnp.bfloat16)
    grads_out = by_transpose(branch_gradient, w_out).astype(jnp.bfloat16)
    if by_pairs:
        (do_own,) = (to_pairs([grads_out], seqs, block),)
        back = attend_back(triple, do_own, attn_wide, lse, cosine, sine)
        d_qp, d_kp, d_vp = from_pairs(back, seqs, block, 3)
    else:
        d_qp, d_kp, d_vp = ring_backward(grads_out, saved)

    f_part = jnp.dot(hidden_state, w_down, preferred_element_type=jnp.float32).astype(BF16)
    f_sum = tp_sum([f_part[s * block : (s + 1) * block] for s in range(seqs)])
    output = h2 + jnp.concatenate(f_sum, axis=0).astype(F32)
    g_out = grad_columns(attn_rows, gather_columns(branch_gradient))

    d_n1_part = (
        by_transpose(d_qp, w_query) + by_transpose(d_kp, w_key) + by_transpose(d_vp, w_value)
    )
    gains = jnp.stack(
        [
            jnp.sum(d_n1_part * h_flat * scale_one, axis=0),
            jnp.where(lax.axis_index("tp") == 0, g_ffn_gain, 0.0),
        ]
    )
    d_n1_part = d_n1_part.astype(BF16)
    d_n1_sum = tp_sum([d_n1_part[s * block : (s + 1) * block] for s in range(seqs)])
    g_query = grad_rows(n1_slices, gather_rows(d_qp))
    g_key = grad_rows(n1_slices, gather_rows(d_kp))
    g_value = grad_rows(n1_slices, gather_rows(d_vp))
    gains = column_piece(sum_everywhere(gains), device_index)

    d_n1 = jnp.concatenate(d_n1_sum, axis=0).astype(F32)
    scaled_one = d_n1 * attn_gain
    d_input = (
        d_h2
        + scale_one * scaled_one
        - h_flat * scale_one**3 * jnp.mean(scaled_one * h_flat, axis=-1, keepdims=True)
    )
    return (
        output.astype(jnp.bfloat16).reshape(seqs, block, width),
        d_input.reshape(seqs, block, width),
        gains[0],
        g_query,
        g_key,
        g_value,
        g_out,
        gains[1],
        g_gate,
        g_up,
        g_down,
    )


def solution(mesh):
    in_specs = (
        P(None, "ctx", None),
        P(),
        P(None, "tp"),
        P(None, "tp"),
        P(None, "tp"),
        P("tp", None),
        P(),
        P(None, "tp"),
        P(None, "tp"),
        P("tp", None),
        P(None, "ctx", None),
    )
    out_specs = (
        P(None, "ctx", None),
        P(None, "ctx", None),
        P("ctx"),
        P("ctx", "tp"),
        P("ctx", "tp"),
        P("ctx", "tp"),
        P("tp", "ctx"),
        P("ctx"),
        P("ctx", "tp"),
        P("ctx", "tp"),
        P("tp", "ctx"),
    )
    return jax.shard_map(
        per_device, mesh=mesh, in_specs=in_specs, out_specs=out_specs, check_vma=False
    )
```
